32 devices in a mesh: subj: 8 (over y, x, core), slab: 4 (over z).
Axes of the slice: x: 2, y: 2, z: 4, core: 2. Of those that a mesh axis runs over, the one named last changes fastest.
Arguments:
- density: bfloat16 [8, 96, 128, 128], P('subj', 'slab'), may hold values from 0.19921875 to 5
- scaling: float32 [8, 96, 128, 128], P('subj', 'slab'), may hold values from 0.5 to 2
- ages: int32 [8], replicated, may hold values from 0 to 3, as said below
Outputs:
- new_scaling: float32 [8, 96, 128, 128], P('subj', 'slab')
- templates: float32 [4, 96, 128, 128], P(None, 'slab', 'subj')
The draws below stay inside these ranges and needn't reach their ends.
Inputs may be any that keep to these rules, and one draw needn't show every extreme that they name: `ages`: every age from 0 to 3 is held by at least one subject.
All inputs are finite; a program needn't handle non-finite values.
Results may differ from the reference program's by a relative error of at most 0.0003.
Values may be sent and summed in bfloat16 or wider, within the bound.
No kernel may reach another device: no remote copies, remote signals or barrier semaphores. Data moves between devices by JAX's collectives and lax.ppermute only.
A program may use at most 64 MiB of HBM per device.

```python
import math
import jax
import jax.numpy as jnp
from jax import lax

X = 128
Y = 128
Z = 96
RADIUS = 4
ITERS = 2
SUBJECTS = 8
BANDS = 4


def draw_ages(key, part):
    key_order, key_one, key_two = jax.random.split(key, 3)
    ordering = jax.random.permutation(key_order, SUBJECTS)
    draw_one = jax.random.randint(key_one, (SUBJECTS,), 0, BANDS)
    draw_two = jax.random.randint(key_two, (SUBJECTS,), 0, BANDS)
    skewed = jnp.minimum(draw_one, draw_two)
    return jnp.where(ordering < BANDS, ordering, skewed).astype(jnp.int32)


def block_scale(stream_key, dims, cuts, smallest, high):
    gain = 1.0
    for axis_at, shards_of in cuts:
        steps = jax.random.uniform(jax.random.fold_in(jax.random.fold_in(stream_key, 6), axis_at), (shards_of,), jnp.float32, smallest / len(cuts), high / len(cuts))
        gain = gain * jnp.repeat(jnp.exp(steps), dims[axis_at] // shards_of).reshape((-1,) + (1,) * (len(dims) - 1 - axis_at))
    return gain


def setup_inputs(seed: int = 0) -> dict:
    keys = jax.random.split(jax.random.key(seed), 4)
    return {
        "density": jnp.clip(jnp.exp(math.log(5.0) - 3.2227897 * jax.random.uniform(keys[0], (SUBJECTS, Z, X, Y), jnp.float32) ** block_scale(keys[0], (SUBJECTS, Z, X, Y), ((0, 8), (1, 4)), -0.2, 0.2)), 0.19921875, 5.0).astype(jnp.bfloat16),
        "scaling": jnp.clip(jnp.exp(math.log(2.0) - 1.3862944 * jax.random.uniform(keys[1], (SUBJECTS, Z, X, Y), jnp.float32) ** block_scale(keys[1], (SUBJECTS, Z, X, Y), ((0, 8), (1, 4)), -0.2, 0.2)), 0.5, 2.0),
        "ages": draw_ages(jax.random.fold_in(keys[3], 71), 0),
    }


highest = lax.Precision.HIGHEST
kernel_spread = 1.5

def gauss_matrix(length):
    points = jnp.arange(length, dtype=jnp.float32)
    offset = points[:, None] - points[None, :]
    values = jnp.exp(-offset * offset / (2.0 * kernel_spread * kernel_spread)) / (math.sqrt(2.0 * math.pi) * kernel_spread)
    return jnp.where(jnp.abs(offset) <= RADIUS, values, jnp.zeros_like(values))

def blur_field(field, kernel_z, kernel_x, kernel_y):
    across = jnp.einsum('zxy,ax->zay', field, kernel_x, precision=highest)
    across = jnp.einsum('zxy,by->zxb', across, kernel_y, precision=highest)
    return jnp.einsum('zxy,cz->cxy', across, kernel_z, precision=highest)

def reference(density, scaling, ages):
    kernel_z = gauss_matrix(Z)
    kernel_x = gauss_matrix(X)
    kernel_y = gauss_matrix(Y)
    band_ids = jnp.arange(BANDS, dtype=jnp.int32)
    member = (jnp.abs(ages[:, None] - band_ids[None, :]) <= 1).astype(jnp.float32)
    band_count = lax.optimization_barrier(jnp.sum(member, axis=0))
    subject_count = lax.optimization_barrier(jnp.sum(member, axis=1))

    def subject_logs(pair):
        dens, value = pair
        blurred = blur_field(value, kernel_z, kernel_x, kernel_y)
        weight = dens.astype(jnp.float32) / blurred
        return jnp.log(value * blur_field(weight, kernel_z, kernel_x, kernel_y))
    value = scaling
    log_template = jnp.zeros((BANDS, Z, X, Y), jnp.float32)
    for iteration in range(ITERS):
        log_d = lax.map(subject_logs, (density, value))
        log_template = jnp.einsum('sb,szxy->bzxy', member, log_d, precision=highest) / band_count[:, None, None, None]
        log_target = jnp.einsum('sb,bzxy->szxy', member, log_template, precision=highest) / subject_count[:, None, None, None]
        value = value * jnp.exp(log_target - log_d)
    return (value, jnp.exp(log_template))
```

```python
import functools
import math

import jax
import jax.numpy as jnp
from jax import lax
from jax.experimental import pallas as pl
from jax.experimental.pallas import tpu as pltpu
from jax.sharding import PartitionSpec as P

RADIUS = 4
ITERS = 2
GROUP = 4
SPREAD = 1.5
LOG_SCALE = 2048.0
CODE_MAX = 32767.0
V_MID = 1.25
V_SCALE = 32767.0 / 0.75
DENSITY_SCALE = 1024.0


TAPS = [
    math.exp(-k * k / (2.0 * SPREAD * SPREAD)) / (math.sqrt(2.0 * math.pi) * SPREAD)
    for k in range(RADIUS + 1)
]


def gauss_matrix(length):
    points = jnp.arange(length, dtype=jnp.float32)
    offset = points[:, None] - points[None, :]
    values = jnp.exp(-offset * offset / (2.0 * SPREAD * SPREAD)) / (math.sqrt(2.0 * math.pi) * SPREAD)
    return jnp.where(jnp.abs(offset) <= RADIUS, values, jnp.zeros_like(values))


def split(x):
    hi = x.astype(jnp.bfloat16)
    lo = (x - hi.astype(jnp.float32)).astype(jnp.bfloat16)
    return hi, lo


def blur_operands(rows, cols):
    xh, xl = split(gauss_matrix(rows))
    yh, yl = split(gauss_matrix(cols))
    left = jnp.concatenate(
        [jnp.concatenate([xh, xh], 1), jnp.concatenate([xl, jnp.zeros_like(xl)], 1)], 0
    )
    right = jnp.concatenate(
        [jnp.concatenate([yh, yl], 1), jnp.concatenate([yh, jnp.zeros_like(yl)], 1)], 0
    )
    return left, right


def encode(x, scale):
    return jnp.clip(jnp.round(x * scale), -CODE_MAX, CODE_MAX).astype(jnp.int32).astype(jnp.int16)


def decode(code):
    return code.astype(jnp.int32).astype(jnp.float32)


def depth_blur(ref, first):
    planes = [ref[first + i] for i in range(GROUP + 2 * RADIUS)]
    out = []
    for j in range(GROUP):
        total = TAPS[0] * planes[j + RADIUS]
        for k in range(1, RADIUS + 1):
            total += TAPS[k] * (planes[j + RADIUS - k] + planes[j + RADIUS + k])
        out.append(total)
    return out


def blur_group(ref, first, left_ref, right_ref):
    planes = depth_blur(ref, first)
    rows, cols = planes[0].shape
    left = left_ref[...]
    across = []
    for j in range(0, GROUP, 2):
        pair = [split(planes[j]), split(planes[j + 1])]
        rhs = jnp.concatenate(
            [
                jnp.concatenate([pair[0][0], pair[1][0]], 1),
                jnp.concatenate([pair[0][1], pair[1][1]], 1),
            ],
            0,
        )
        both = jnp.dot(left, rhs, preferred_element_type=jnp.float32)
        both = both[:rows] + both[rows:]
        across += [both[:, :cols], both[:, cols:]]
    lhs = jnp.concatenate([jnp.concatenate(split(a), 1) for a in across], 0)
    out = jnp.dot(lhs, right_ref[...], preferred_element_type=jnp.float32)
    out = out[:, :cols] + out[:, cols:]
    return [out[j * rows : (j + 1) * rows] for j in range(GROUP)]


def halo_places(slabs, planes, halo):
    slab = lax.axis_index("slab")
    even = lax.rem(slab, 2) == 0
    below = planes + halo
    first = (jnp.where(even, below, 0), jnp.where(even, slab + 1 < slabs, True))
    second = (jnp.where(even, 0, below), jnp.where(even, slab > 0, slab + 1 < slabs))
    return first, second


def logs_kernel(
    parts, slabs, coded_log,
    v_ref, va_ref, vb_ref, dens_ref, da_ref, db_ref, left_ref, right_ref, *rest,
):
    outs, logk_ref, vext, dext, weight = rest[:parts], rest[parts], rest[-3], rest[-2], rest[-1]
    planes, rows, _ = v_ref.shape
    halo = 2 * RADIUS
    vext[halo : halo + planes] = v_ref[...]
    dext[RADIUS : RADIUS + planes] = dens_ref[...].astype(jnp.float32)
    v_places = halo_places(slabs, planes, halo)
    d_places = halo_places(slabs, planes, RADIUS)
    for (place, there), code_ref in zip(v_places, (va_ref, vb_ref)):
        gate = jnp.where(there, 1.0, 0.0)

        def fill(i, carry, place=place, gate=gate, code_ref=code_ref):
            value = decode(code_ref[i])
            if coded_log:
                value = jnp.exp(value * (1.0 / LOG_SCALE))
            else:
                value = value * (1.0 / V_SCALE) + V_MID
            vext[place + i] = value * gate
            return carry

        lax.fori_loop(0, halo, fill, 0)
    for (place, there), code_ref in zip(d_places, (da_ref, db_ref)):
        gate = jnp.where(there, 1.0 / DENSITY_SCALE, 0.0)

        def fill(i, carry, place=place, gate=gate, code_ref=code_ref):
            dext[place + i] = decode(code_ref[i]) * gate
            return carry

        lax.fori_loop(0, RADIUS, fill, 0)

    def weights(g, carry):
        first = g * GROUP
        for j, blurred in enumerate(blur_group(vext, first, left_ref, right_ref)):
            weight[first + j] = dext[first + j] / blurred
        return carry

    lax.fori_loop(0, (planes + 2 * RADIUS) // GROUP, weights, 0)

    me = lax.axis_index("subj")
    part_rows = rows // parts

    def logs(g, carry):
        first = g * GROUP
        for j, blurred in enumerate(blur_group(weight, first, left_ref, right_ref)):
            logk_ref[first + j] = jnp.log(blurred)
        for k in range(parts):
            at = pl.ds(pl.multiple_of((me ^ k) * part_rows, part_rows), part_rows)
            some = pl.ds(first, GROUP)
            log_d = jnp.log(v_ref[some, at, :]) + logk_ref[some, at, :]
            outs[k][some] = encode(log_d, LOG_SCALE)
        return carry

    lax.fori_loop(0, planes // GROUP, logs, 0)


def mix_kernel(parts, bands, last, into_ref, from_ref, *rest):
    ins, outs = rest[:parts], rest[parts : 2 * parts]
    planes = ins[0].shape[0]
    step = 2

    def some(g, carry):
        at = pl.ds(g * step, step)
        logs = [decode(ref[at]) for ref in ins]
        templates = []
        for b in range(bands):
            total = into_ref[b, 0] * logs[0]
            for k in range(1, parts):
                total += into_ref[b, k] * logs[k]
            templates.append(total)
            if last:
                rest[2 * parts][b, at] = jnp.exp(total * (1.0 / LOG_SCALE))
        for k in range(parts):
            total = from_ref[k, 0] * templates[0]
            for b in range(1, bands):
                total += from_ref[k, b] * templates[b]
            outs[k][at] = encode(total, 1.0)
        return carry

    lax.fori_loop(0, planes // step, some, 0)


def target_kernel(parts, halos, logk_ref, *rest):
    ins, v_ref = rest[:parts], rest[parts]
    planes, rows, _ = v_ref.shape
    me = lax.axis_index("subj")
    part_rows = rows // parts
    halo = 2 * RADIUS
    if halos:
        slab = lax.axis_index("slab")
        even = lax.rem(slab, 2) == 0
        firsts = (jnp.where(even, planes - halo, 0), jnp.where(even, 0, planes - halo))
    for k in range(parts):
        at = pl.ds(pl.multiple_of((me ^ k) * part_rows, part_rows), part_rows)
        log_v = decode(ins[k][...]) * (1.0 / LOG_SCALE) - logk_ref[:, at, :]
        v_ref[:, at, :] = jnp.exp(log_v)
        if halos:
            for first, out_ref in zip(firsts, rest[parts + 1 :]):
                some = pl.ds(first, halo)
                log_v = decode(ins[k][some]) * (1.0 / LOG_SCALE) - logk_ref[some, at, :]
                out_ref[:, at, :] = encode(log_v, LOG_SCALE)


VMEM = pl.BlockSpec(memory_space=pltpu.VMEM)
SMEM = pl.BlockSpec(memory_space=pltpu.SMEM)


def per_device_small(density, scaling, ages):
    parts = lax.axis_size("subj")
    slabs = lax.axis_size("slab")
    density, value = density[0], scaling[0]
    planes, rows, cols = value.shape
    part_rows = rows // parts
    halo = 2 * RADIUS
    f32 = jnp.float32
    left, right = blur_operands(rows, cols)

    bands = ages.shape[0] // 2
    band_ids = jnp.arange(bands, dtype=jnp.int32)
    member = (jnp.abs(ages[:, None] - band_ids[None, :]) <= 1).astype(f32)
    relative = lax.axis_index("subj") ^ jnp.arange(parts, dtype=jnp.int32)
    near = (jnp.abs(ages[relative][:, None] - band_ids[None, :]) <= 1).astype(f32)
    into = near.T / jnp.sum(member, axis=0)[:, None]
    back = near / jnp.sum(near, axis=1)[:, None]

    even = lax.rem(lax.axis_index("slab"), 2) == 0
    even_pairs = [(i, i ^ 1) for i in range(slabs) if (i ^ 1) < slabs]
    odd_pairs = [(i, i + 1) for i in range(1, slabs - 1, 2)]
    odd_pairs += [(b, a) for a, b in odd_pairs]

    def ends(x, size):
        top, bottom = x[:size], x[planes - size :]
        return jnp.where(even, bottom, top), jnp.where(even, top, bottom)

    def swap(a, b):
        return lax.ppermute(a, "slab", even_pairs), lax.ppermute(b, "slab", odd_pairs)

    def exchange(pieces):
        return [pieces[0]] + [
            lax.ppermute(pieces[k], "subj", [(i, i ^ k) for i in range(parts)])
            for k in range(1, parts)
        ]

    piece = jax.ShapeDtypeStruct((planes, part_rows, cols), jnp.int16)
    field = jax.ShapeDtypeStruct((planes, rows, cols), f32)
    edge = jax.ShapeDtypeStruct((halo, rows, cols), jnp.int16)

    def logs(coded_log, value, va, vb, da, db):
        out = pl.pallas_call(
            functools.partial(logs_kernel, parts, slabs, coded_log),
            out_shape=[piece] * parts + [field],
            in_specs=[VMEM] * 8,
            out_specs=[VMEM] * (parts + 1),
            scratch_shapes=[
                pltpu.VMEM((planes + 2 * halo, rows, cols), f32),
                pltpu.VMEM((planes + halo, rows, cols), f32),
                pltpu.VMEM((planes + halo, rows, cols), f32),
            ],
            compiler_params=pltpu.CompilerParams(vmem_limit_bytes=40 << 20),
        )(value, va, vb, density, da, db, left, right)
        return out[:parts], out[parts]

    def mix(pieces, last):
        template = jax.ShapeDtypeStruct((bands, planes, part_rows, cols), f32)
        out = pl.pallas_call(
            functools.partial(mix_kernel, parts, bands, last),
            out_shape=[piece] * parts + ([template] if last else []),
            in_specs=[SMEM] * 2 + [VMEM] * parts,
            out_specs=[VMEM] * (parts + last),
        )(into, back, *pieces)
        return out[:parts], out[-1]

    def target(logk, pieces, halos):
        return pl.pallas_call(
            functools.partial(target_kernel, parts, halos),
            out_shape=[field] + ([edge] * 2 if halos else []),
            in_specs=[VMEM] * (parts + 1),
            out_specs=[VMEM] * (3 if halos else 1),
        )(logk, *pieces)

    v_ends = [encode(e - V_MID, V_SCALE) for e in ends(value, halo)]
    d_ends = [encode(e.astype(f32), DENSITY_SCALE) for e in ends(density, RADIUS)]
    first = swap(*[jnp.concatenate(pair, 0) for pair in zip(v_ends, d_ends)])
    da, db = [got[halo:] for got in first]
    va, vb = [got[:halo] for got in first]
    templates = None
    for iteration in range(ITERS):
        last = iteration == ITERS - 1
        pieces, logk = logs(iteration > 0, value, va, vb, da, db)
        back_pieces, templates = mix(exchange(pieces), last)
        out = target(logk, exchange(back_pieces), not last)
        value = out[0]
        if not last:
            va, vb = swap(out[1], out[2])
    return value[None], templates


highest = lax.Precision.HIGHEST


def per_device_large(density, scaling, ages):
    planes_local = density.shape[1]
    depth = planes_local * lax.axis_size("slab")
    kernel_z = gauss_matrix(depth)
    kernel_x = gauss_matrix(density.shape[2])
    kernel_y = gauss_matrix(density.shape[3])
    bands = ages.shape[0] // 2
    band_ids = jnp.arange(bands, dtype=jnp.int32)
    member = (jnp.abs(ages[:, None] - band_ids[None, :]) <= 1).astype(jnp.float32)
    band_count = jnp.sum(member, axis=0)
    subject_count = jnp.sum(member, axis=1)

    def blur_full(field):
        planar = jnp.einsum("szxy,ax->szay", field, kernel_x, precision=highest)
        planar = jnp.einsum("szxy,by->szxb", planar, kernel_y, precision=highest)
        columns = lax.all_to_all(planar, "slab", split_axis=2, concat_axis=1, tiled=True)
        columns = jnp.einsum("szxy,cz->scxy", columns, kernel_z, precision=highest)
        return lax.all_to_all(columns, "slab", split_axis=1, concat_axis=2, tiled=True)

    value = scaling
    log_template = None
    for iteration in range(ITERS):
        weight = density.astype(jnp.float32) / blur_full(value)
        log_d = jnp.log(value * blur_full(weight))
        gathered = lax.all_to_all(log_d, "subj", split_axis=2, concat_axis=0, tiled=True)
        log_template = (
            jnp.einsum("sb,szxy->bzxy", member, gathered, precision=highest)
            / band_count[:, None, None, None]
        )
        log_target = (
            jnp.einsum("sb,bzxy->szxy", member, log_template, precision=highest)
            / subject_count[:, None, None, None]
        )
        target_home = lax.all_to_all(log_target, "subj", split_axis=0, concat_axis=2, tiled=True)
        value = value * jnp.exp(target_home - log_d)
    return (value, jnp.exp(log_template))


def per_device(density, scaling, ages):
    parts = lax.axis_size("subj")
    planes, rows = scaling.shape[1:3]
    one_subject = scaling.shape[0] == 1 and parts & (parts - 1) == 0
    whole_tiles = rows % (16 * parts) == 0 and planes % GROUP == 0 and planes >= 2 * RADIUS
    if one_subject and whole_tiles and lax.axis_size("slab") % 2 == 0:
        return per_device_small(density, scaling, ages)
    return per_device_large(density, scaling, ages)


def solution(mesh):
    in_specs = (P("subj", "slab", None, None), P("subj", "slab", None, None), P())
    out_specs = (P("subj", "slab", None, None), P(None, "slab", "subj", None))
    return jax.shard_map(
        per_device, mesh=mesh, in_specs=in_specs, out_specs=out_specs, check_vma=False
    )
```

```python
import functools
import math

import jax
import jax.numpy as jnp
from jax import lax
from jax.experimental import pallas as pl
from jax.experimental.pallas import tpu as pltpu
from jax.sharding import PartitionSpec as P

RADIUS = 4
ITERS = 2
GROUP = 4
SPREAD = 1.5
LOG_SCALE = 2048.0
CODE_MAX = 32767.0
V_MID = 1.25
V_SCALE = 32767.0 / 0.75
DENSITY_SCALE = 1024.0


TAPS = [
    math.exp(-k * k / (2.0 * SPREAD * SPREAD)) / (math.sqrt(2.0 * math.pi) * SPREAD)
    for k in range(RADIUS + 1)
]


def gauss_matrix(length):
    points = jnp.arange(length, dtype=jnp.float32)
    offset = points[:, None] - points[None, :]
    values = jnp.exp(-offset * offset / (2.0 * SPREAD * SPREAD)) / (math.sqrt(2.0 * math.pi) * SPREAD)
    return jnp.where(jnp.abs(offset) <= RADIUS, values, jnp.zeros_like(values))


def split(x):
    hi = x.astype(jnp.bfloat16)
    lo = (x - hi.astype(jnp.float32)).astype(jnp.bfloat16)
    return hi, lo


def blur_operands(rows, cols):
    xh, xl = split(gauss_matrix(rows))
    yh, yl = split(gauss_matrix(cols))
    left = jnp.concatenate(
        [jnp.concatenate([xh, xh], 1), jnp.concatenate([xl, jnp.zeros_like(xl)], 1)], 0
    )
    right = jnp.concatenate(
        [jnp.concatenate([yh, yl], 1), jnp.concatenate([yh, jnp.zeros_like(yl)], 1)], 0
    )
    return left, right


def encode(x, scale):
    return jnp.clip(jnp.round(x * scale), -CODE_MAX, CODE_MAX).astype(jnp.int32).astype(jnp.int16)


def decode(code):
    return code.astype(jnp.int32).astype(jnp.float32)


def depth_blur(ref, first):
    planes = [ref[first + i] for i in range(GROUP + 2 * RADIUS)]
    out = []
    for j in range(GROUP):
        total = TAPS[0] * planes[j + RADIUS]
        for k in range(1, RADIUS + 1):
            total += TAPS[k] * (planes[j + RADIUS - k] + planes[j + RADIUS + k])
        out.append(total)
    return out


def cross_blur(planes, left):
    rows, cols = planes[0].shape
    across = []
    for j in range(0, GROUP, 2):
        pair = [split(planes[j]), split(planes[j + 1])]
        rhs = jnp.concatenate(
            [
                jnp.concatenate([pair[0][0], pair[1][0]], 1),
                jnp.concatenate([pair[0][1], pair[1][1]], 1),
            ],
            0,
        )
        both = jnp.dot(left, rhs, preferred_element_type=jnp.float32)
        both = both[:rows] + both[rows:]
        across += [both[:, :cols], both[:, cols:]]
    return jnp.concatenate([jnp.concatenate(split(a), 1) for a in across], 0)


def along_blur(lhs, right):
    rows, cols = lhs.shape[0] // GROUP, lhs.shape[1] // 2
    out = jnp.dot(lhs, right, preferred_element_type=jnp.float32)
    out = out[:, :cols] + out[:, cols:]
    return [out[j * rows : (j + 1) * rows] for j in range(GROUP)]


def blur_loop(count, read, finish, half_ref, left_ref, right_ref, after=None):
    def begin(i):
        ref, first = read(i)
        half_ref[...] = cross_blur(depth_blur(ref, first), left_ref[...])

    def end(i):
        finish(i, along_blur(half_ref[...], right_ref[...]))

    begin(0)

    def step(i, carry):
        if after is not None:
            after(i - 2)
        end(i - 1)
        begin(i)
        return carry

    if after is None:
        lax.fori_loop(1, count, step, 0)
        end(count - 1)
    else:
        end(0)
        begin(1)
        lax.fori_loop(2, count, step, 0)
        after(count - 2)
        end(count - 1)
        after(count - 1)


def inner_kernel(v_ref, dens_ref, left_ref, right_ref, weight_ref, logk_ref, half_ref):
    def weights(i, blurred):
        for j in range(GROUP):
            at = i * GROUP + j
            weight_ref[at] = dens_ref[at + RADIUS].astype(jnp.float32) / blurred[j]

    def logs(i, blurred):
        for j in range(GROUP):
            logk_ref[i * GROUP + j] = jnp.log(blurred[j])

    blur_loop(
        weight_ref.shape[0] // GROUP, lambda i: (v_ref, i * GROUP), weights,
        half_ref, left_ref, right_ref,
    )
    blur_loop(
        logk_ref.shape[0] // GROUP, lambda i: (weight_ref, i * GROUP), logs,
        half_ref, left_ref, right_ref,
    )


def logs_kernel(
    parts, slabs, coded_log,
    v_ref, va_ref, vb_ref, dens_ref, da_ref, db_ref, inner_ref, inner_logk_ref,
    left_ref, right_ref, *rest,
):
    outs, logk_ref = rest[:parts], rest[parts]
    vext, dext, weight, half_ref = rest[parts + 1 :]
    planes, rows, _ = v_ref.shape
    halo = 2 * RADIUS
    slab = lax.axis_index("slab")
    even = lax.rem(slab, 2) == 0
    there = (
        jnp.where(even, slab + 1 < slabs, True),
        jnp.where(even, slab > 0, slab + 1 < slabs),
    )
    vext[halo : 2 * halo] = v_ref[:halo]
    vext[2 * halo : 3 * halo] = v_ref[planes - halo :]
    dext[RADIUS : 2 * RADIUS] = dens_ref[:RADIUS].astype(jnp.float32)
    dext[2 * RADIUS : 3 * RADIUS] = dens_ref[planes - RADIUS :].astype(jnp.float32)
    weight[halo : planes] = inner_ref[...]
    logk_ref[halo : planes - halo] = inner_logk_ref[...]
    for side, (v_code, d_code) in enumerate(((va_ref, da_ref), (vb_ref, db_ref))):
        above = even if side else jnp.logical_not(even)
        v_place = jnp.where(above, 0, 3 * halo)
        d_place = jnp.where(above, 0, 3 * RADIUS)
        gate = jnp.where(there[side], 1.0, 0.0)

        def fill(i, carry, v_place=v_place, gate=gate, v_code=v_code):
            value = decode(v_code[i])
            if coded_log:
                value = jnp.exp(value * (1.0 / LOG_SCALE))
            else:
                value = value * (1.0 / V_SCALE) + V_MID
            vext[v_place + i] = value * gate
            return carry

        lax.fori_loop(0, halo, fill, 0)
        d_first = d_code.shape[0] - RADIUS
        gate = gate * (1.0 / DENSITY_SCALE)
        for i in range(RADIUS):
            dext[d_place + i] = decode(d_code[d_first + i]) * gate

    edge = halo // GROUP
    total = planes // GROUP

    def read_v(i):
        return vext, jnp.where(i < edge, i, i + edge) * GROUP

    def weights(i, blurred):
        base = jnp.where(i < edge, i, i + total - edge) * GROUP
        for j in range(GROUP):
            weight[base + j] = dext[i * GROUP + j] / blurred[j]

    blur_loop(2 * edge, read_v, weights, half_ref, left_ref, right_ref)

    me = lax.axis_index("subj")
    part_rows = rows // parts

    def place(i):
        return jnp.where(i < edge, i, i + total - 2 * edge) * GROUP

    def logs(i, blurred):
        for j in range(GROUP):
            logk_ref[place(i) + j] = jnp.log(blurred[j])

    def send(first):
        for k in range(parts):
            at = pl.ds(pl.multiple_of((me ^ k) * part_rows, part_rows), part_rows)
            some = pl.ds(first, GROUP)
            log_d = jnp.log(v_ref[some, at, :]) + logk_ref[some, at, :]
            outs[k][some] = encode(log_d, LOG_SCALE)

    def send_inner(i, carry):
        send((i + edge) * GROUP)
        return carry

    lax.fori_loop(0, total - 2 * edge, send_inner, 0)
    blur_loop(
        2 * edge, lambda i: (weight, place(i)), logs, half_ref, left_ref, right_ref,
        after=lambda i: send(place(i)),
    )


def mix_kernel(parts, bands, last, into_ref, from_ref, *rest):
    ins, outs = rest[:parts], rest[parts : 2 * parts]
    planes = ins[0].shape[0]
    step = 2

    def some(g, carry):
        at = pl.ds(g * step, step)
        logs = [decode(ref[at]) for ref in ins]
        templates = []
        for b in range(bands):
            total = into_ref[b, 0] * logs[0]
            for k in range(1, parts):
                total += into_ref[b, k] * logs[k]
            templates.append(total)
            if last:
                rest[2 * parts][b, at] = jnp.exp(total * (1.0 / LOG_SCALE))
        for k in range(parts):
            total = from_ref[k, 0] * templates[0]
            for b in range(1, bands):
                total += from_ref[k, b] * templates[b]
            outs[k][at] = encode(total, 1.0)
        return carry

    lax.fori_loop(0, planes // step, some, 0)


def target_kernel(parts, halos, logk_ref, *rest):
    ins, v_ref = rest[:parts], rest[parts]
    planes, rows, _ = v_ref.shape
    me = lax.axis_index("subj")
    part_rows = rows // parts
    halo = 2 * RADIUS
    if halos:
        slab = lax.axis_index("slab")
        even = lax.rem(slab, 2) == 0
        firsts = (jnp.where(even, planes - halo, 0), jnp.where(even, 0, planes - halo))
    for k in range(parts):
        at = pl.ds(pl.multiple_of((me ^ k) * part_rows, part_rows), part_rows)
        log_v = decode(ins[k][...]) * (1.0 / LOG_SCALE) - logk_ref[:, at, :]
        v_ref[:, at, :] = jnp.exp(log_v)
        if halos:
            for first, out_ref in zip(firsts, rest[parts + 1 :]):
                some = pl.ds(first, halo)
                log_v = decode(ins[k][some]) * (1.0 / LOG_SCALE) - logk_ref[some, at, :]
                out_ref[:, at, :] = encode(log_v, LOG_SCALE)


VMEM = pl.BlockSpec(memory_space=pltpu.VMEM)
SMEM = pl.BlockSpec(memory_space=pltpu.SMEM)


def per_device_small(density, scaling, ages):
    parts = lax.axis_size("subj")
    slabs = lax.axis_size("slab")
    density, value = density[0], scaling[0]
    planes, rows, cols = value.shape
    part_rows = rows // parts
    halo = 2 * RADIUS
    f32 = jnp.float32
    left, right = blur_operands(rows, cols)

    bands = ages.shape[0] // 2
    band_ids = jnp.arange(bands, dtype=jnp.int32)
    member = (jnp.abs(ages[:, None] - band_ids[None, :]) <= 1).astype(f32)
    relative = lax.axis_index("subj") ^ jnp.arange(parts, dtype=jnp.int32)
    near = (jnp.abs(ages[relative][:, None] - band_ids[None, :]) <= 1).astype(f32)
    into = near.T / jnp.sum(member, axis=0)[:, None]
    back = near / jnp.sum(near, axis=1)[:, None]

    even = lax.rem(lax.axis_index("slab"), 2) == 0
    even_pairs = [(i, i ^ 1) for i in range(slabs) if (i ^ 1) < slabs]
    odd_pairs = [(i, i + 1) for i in range(1, slabs - 1, 2)]
    odd_pairs += [(b, a) for a, b in odd_pairs]

    def ends(x, size):
        top, bottom = x[:size], x[planes - size :]
        return jnp.where(even, bottom, top), jnp.where(even, top, bottom)

    def swap(a, b):
        return lax.ppermute(a, "slab", even_pairs), lax.ppermute(b, "slab", odd_pairs)

    def exchange(pieces):
        return [pieces[0]] + [
            lax.ppermute(pieces[k], "subj", [(i, i ^ k) for i in range(parts)])
            for k in range(1, parts)
        ]

    piece = jax.ShapeDtypeStruct((planes, part_rows, cols), jnp.int16)
    field = jax.ShapeDtypeStruct((planes, rows, cols), f32)
    edge = jax.ShapeDtypeStruct((halo, rows, cols), jnp.int16)

    half = pltpu.VMEM((GROUP * rows, 2 * cols), jnp.bfloat16)

    def logs(coded_log, value, va, vb, da, db):
        weight, inner_logk = pl.pallas_call(
            inner_kernel,
            out_shape=[
                jax.ShapeDtypeStruct((planes - halo, rows, cols), f32),
                jax.ShapeDtypeStruct((planes - 2 * halo, rows, cols), f32),
            ],
            in_specs=[VMEM] * 4,
            out_specs=[VMEM] * 2,
            scratch_shapes=[half],
            compiler_params=pltpu.CompilerParams(vmem_limit_bytes=12 << 20),
            cost_estimate=pl.CostEstimate(
                flops=4 * planes * rows * cols * 512, bytes_accessed=8 << 20, transcendentals=0
            ),
        )(value, density, left, right)
        out = pl.pallas_call(
            functools.partial(logs_kernel, parts, slabs, coded_log),
            out_shape=[piece] * parts + [field],
            in_specs=[VMEM] * 10,
            out_specs=[VMEM] * (parts + 1),
            scratch_shapes=[
                pltpu.VMEM((4 * halo, rows, cols), f32),
                pltpu.VMEM((4 * RADIUS, rows, cols), f32),
                pltpu.VMEM((planes + halo, rows, cols), f32),
                half,
            ],
            compiler_params=pltpu.CompilerParams(vmem_limit_bytes=20 << 20),
        )(value, va, vb, density, da, db, weight, inner_logk, left, right)
        return out[:parts], out[parts]

    def mix(pieces, last):
        template = jax.ShapeDtypeStruct((bands, planes, part_rows, cols), f32)
        out = pl.pallas_call(
            functools.partial(mix_kernel, parts, bands, last),
            out_shape=[piece] * parts + ([template] if last else []),
            in_specs=[SMEM] * 2 + [VMEM] * parts,
            out_specs=[VMEM] * (parts + last),
            compiler_params=pltpu.CompilerParams(vmem_limit_bytes=8 << 20),
        )(into, back, *pieces)
        return out[:parts], out[-1]

    def target(logk, pieces, halos):
        return pl.pallas_call(
            functools.partial(target_kernel, parts, halos),
            out_shape=[field] + ([edge] * 2 if halos else []),
            in_specs=[VMEM] * (parts + 1),
            out_specs=[VMEM] * (3 if halos else 1),
            compiler_params=pltpu.CompilerParams(vmem_limit_bytes=10 << 20),
        )(logk, *pieces)

    v_ends = [encode(e - V_MID, V_SCALE) for e in ends(value, halo)]
    d_ends = [encode(e.astype(f32), DENSITY_SCALE) for e in ends(density, RADIUS)]
    da, db = swap(*[jnp.concatenate(pair, 0) for pair in zip(v_ends, d_ends)])
    va, vb = da, db
    templates = None
    for iteration in range(ITERS):
        last = iteration == ITERS - 1
        pieces, logk = logs(iteration > 0, value, va, vb, da, db)
        back_pieces, templates = mix(exchange(pieces), last)
        out = target(logk, exchange(back_pieces), not last)
        value = out[0]
        if not last:
            va, vb = swap(out[1], out[2])
    return value[None], templates


highest = lax.Precision.HIGHEST


def per_device_large(density, scaling, ages):
    planes_local = density.shape[1]
    depth = planes_local * lax.axis_size("slab")
    kernel_z = gauss_matrix(depth)
    kernel_x = gauss_matrix(density.shape[2])
    kernel_y = gauss_matrix(density.shape[3])
    bands = ages.shape[0] // 2
    band_ids = jnp.arange(bands, dtype=jnp.int32)
    member = (jnp.abs(ages[:, None] - band_ids[None, :]) <= 1).astype(jnp.float32)
    band_count = jnp.sum(member, axis=0)
    subject_count = jnp.sum(member, axis=1)

    def blur_full(field):
        planar = jnp.einsum("szxy,ax->szay", field, kernel_x, precision=highest)
        planar = jnp.einsum("szxy,by->szxb", planar, kernel_y, precision=highest)
        columns = lax.all_to_all(planar, "slab", split_axis=2, concat_axis=1, tiled=True)
        columns = jnp.einsum("szxy,cz->scxy", columns, kernel_z, precision=highest)
        return lax.all_to_all(columns, "slab", split_axis=1, concat_axis=2, tiled=True)

    value = scaling
    log_template = None
    for iteration in range(ITERS):
        weight = density.astype(jnp.float32) / blur_full(value)
        log_d = jnp.log(value * blur_full(weight))
        gathered = lax.all_to_all(log_d, "subj", split_axis=2, concat_axis=0, tiled=True)
        log_template = (
            jnp.einsum("sb,szxy->bzxy", member, gathered, precision=highest)
            / band_count[:, None, None, None]
        )
        log_target = (
            jnp.einsum("sb,bzxy->szxy", member, log_template, precision=highest)
            / subject_count[:, None, None, None]
        )
        target_home = lax.all_to_all(log_target, "subj", split_axis=0, concat_axis=2, tiled=True)
        value = value * jnp.exp(target_home - log_d)
    return (value, jnp.exp(log_template))


def per_device(density, scaling, ages):
    parts = lax.axis_size("subj")
    planes, rows = scaling.shape[1:3]
    one_subject = scaling.shape[0] == 1 and parts & (parts - 1) == 0
    whole_tiles = rows % (16 * parts) == 0 and planes % GROUP == 0 and planes >= 6 * RADIUS
    if one_subject and whole_tiles and lax.axis_size("slab") % 2 == 0:
        return per_device_small(density, scaling, ages)
    return per_device_large(density, scaling, ages)


def solution(mesh):
    in_specs = (P("subj", "slab", None, None), P("subj", "slab", None, None), P())
    out_specs = (P("subj", "slab", None, None), P(None, "slab", "subj", None))
    return jax.shard_map(
        per_device, mesh=mesh, in_specs=in_specs, out_specs=out_specs, check_vma=False
    )
```
